32 devices in a mesh: orb: 8 (over z, x), grid: 4 (over y, core).
Axes of the slice: x: 2, y: 2, z: 4, core: 2. Of those that a mesh axis runs over, the one named last changes fastest.
Arguments:
- potentials: float32 [8, 2, 4, 64, 1024], P('orb', None, None, 'grid'), may hold values from -6 to 6
- orbitals: float32 [32, 64, 1024], P('orb', 'grid'), may hold values from -6 to 6
- local_pot: float32 [64, 1024], P('grid'), may hold values from 0 to 1
- shifts: float32 [32], P('orb'), may hold values from 0.75 to 2
- occupation: int32 [32], P('orb'), may hold values from 1 to 2
- owner: int32 [2], replicated, may hold values from 0 to 7
Outputs:
- response: float32 [8, 2, 4, 64, 1024], P('orb', None, None, 'grid')
The draws below stay inside these ranges and needn't reach their ends.
All inputs are finite; a program needn't handle non-finite values.
Results may differ from the reference program's by a relative error of at most 0.00002.
Values sent between devices are 32-bit elements; how exact they have to be, the bound alone decides.
A program may use at most 64 MiB of HBM per device.

```python
import math
import jax
import jax.numpy as jnp
from jax import lax

NZ = 32
TRIAL = 4
BLOCKS = 2
ITERS = 4
PLANE = 1024
NX = 64
ORBITALS = 32
SLOTS = 8


def place_ends(array, rng, least, top_value):
    index_at = [jax.random.randint(jax.random.fold_in(rng, axis), (), 0, length) for axis, length in enumerate(array.shape)]
    main_axis = array.shape.index(max(array.shape))
    next_to = index_at[:main_axis] + [(index_at[main_axis] + 1) % array.shape[main_axis]] + index_at[main_axis + 1:]
    return array.at[tuple(index_at)].set(least).at[tuple(next_to)].set(top_value)


def levels(rng, extent, cuts, smallest, largest):
    loudness = 1.0
    for position, parts in cuts:
        steps = jax.random.uniform(jax.random.fold_in(jax.random.fold_in(rng, 6), position), (parts,), jnp.float32, smallest / len(cuts), largest / len(cuts))
        loudness = loudness * jnp.repeat(jnp.exp(steps), extent[position] // parts).reshape((-1,) + (1,) * (len(extent) - 1 - position))
    return loudness


def bell_draw(stream_key, shape, spread, bound, split=(), kind=jnp.bfloat16):
    array = jax.random.normal(stream_key, shape, jnp.float32) * spread
    if len(split) > 0:
        array = levels(stream_key, shape, split, -0.22, 0.18) * array
    return jnp.clip(array, min=-bound, max=bound).astype(kind)


def setup_inputs(seed: int = 0) -> dict:
    keys = jax.random.split(jax.random.key(seed), 7)
    return {
        "potentials": bell_draw(keys[0], (SLOTS, BLOCKS, TRIAL, NX, PLANE), 1.0, 6.0, ((0, 8), (3, 4)), jnp.float32),
        "orbitals": bell_draw(keys[1], (ORBITALS, NX, PLANE), 1.0, 6.0, ((0, 8), (1, 4)), jnp.float32),
        "local_pot": jnp.clip(1.0 * jax.random.uniform(keys[2], (NX, PLANE), jnp.float32) ** levels(keys[2], (NX, PLANE), ((0, 4),), -0.2, 0.2), 0.0, 1.0),
        "shifts": jnp.clip(jnp.exp(math.log(2.0) - 0.98082925 * jax.random.uniform(keys[3], (ORBITALS,), jnp.float32) ** levels(keys[3], (ORBITALS,), ((0, 8),), -0.2, 0.2)), 0.75, 2.0),
        "occupation": place_ends(jax.random.randint(keys[4], (ORBITALS,), 1, 3), jax.random.fold_in(keys[4], 1), 1, 2).astype(jnp.int32),
        "owner": jax.random.randint(keys[5], (BLOCKS,), 0, SLOTS).astype(jnp.int32),
    }


NEAR_COEF = 4.0 / 3.0
FAR_COEF = -1.0 / 12.0
CENTER_COEF = -2.5
KINETIC_DIAG = 3.75


def laplacian(padded, solution):
    cell_rows = solution.shape[-2]
    plane_cells = solution.shape[-1]
    along_rows = NEAR_COEF * (padded[..., 1:cell_rows + 1, :] + padded[..., 3:cell_rows + 3, :]) + FAR_COEF * (padded[..., 0:cell_rows, :] + padded[..., 4:cell_rows + 4, :])
    widths = [(0, 0)] * (solution.ndim - 1)
    padded_cols = jnp.pad(solution, widths + [(2 * NZ, 2 * NZ)])
    along_cols = NEAR_COEF * (padded_cols[..., NZ:NZ + plane_cells] + padded_cols[..., 3 * NZ:3 * NZ + plane_cells]) + FAR_COEF * (padded_cols[..., 0:plane_cells] + padded_cols[..., 4 * NZ:4 * NZ + plane_cells])
    padded_depth = jnp.pad(solution, widths + [(2, 2)])
    z_index = jnp.arange(plane_cells, dtype=jnp.int32) % NZ
    lower_one = (z_index >= 1).astype(solution.dtype)
    upper_one = (z_index <= NZ - 2).astype(solution.dtype)
    lower_two = (z_index >= 2).astype(solution.dtype)
    upper_two = (z_index <= NZ - 3).astype(solution.dtype)
    along_depth = NEAR_COEF * (padded_depth[..., 1:plane_cells + 1] * lower_one + padded_depth[..., 3:plane_cells + 3] * upper_one) + FAR_COEF * (padded_depth[..., 0:plane_cells] * lower_two + padded_depth[..., 4:plane_cells + 4] * upper_two)
    return along_rows + along_cols + along_depth + 3.0 * CENTER_COEF * solution


def sweep(padded, solution, source, potential, diagonal):
    applied = -0.5 * laplacian(padded, solution) + potential * solution
    return solution + (source - applied) / diagonal


def reference(potentials, orbitals, local_pot, shifts, occupation, owner):
    slot_ids = jnp.arange(SLOTS, dtype=jnp.int32)
    chosen_slot = (slot_ids[:, None] == owner[None, :]).astype(jnp.float32)
    block_ids = jnp.arange(BLOCKS, dtype=jnp.int32)
    trials = potentials[owner, block_ids].reshape(BLOCKS * TRIAL, NX, PLANE)

    def one_orbital(accumulated, inputs):
        orbital, shift_value, weight = inputs
        source = -(trials * orbital[None])
        potential = local_pot + shift_value
        diagonal = KINETIC_DIAG + potential
        solution = source / diagonal
        for repeat in range(ITERS):
            padded = jnp.pad(solution, ((0, 0), (2, 2), (0, 0)))
            solution = sweep(padded, solution, source, potential, diagonal)
        return accumulated + weight.astype(jnp.float32) * orbital[None] * solution, None

    start_sum = jnp.zeros((BLOCKS * TRIAL, NX, PLANE), jnp.float32)
    accumulated, unused = lax.scan(one_orbital, start_sum, (orbitals, shifts, occupation))
    density = accumulated.reshape(BLOCKS, TRIAL, NX, PLANE)
    return chosen_slot[:, :, None, None, None] * density[None]
```

```python
import functools

import jax
import jax.numpy as jnp
from jax import lax
from jax.experimental import pallas as pl
from jax.experimental.pallas import tpu as pltpu
from jax.sharding import PartitionSpec as P

NZ = 32
ITERS = 4
REACH = 2
HALO = REACH * ITERS
KINETIC_DIAG = 3.75
PAIR = 2
MESH = pl.DeviceIdType.MESH


class Ring:
    def __init__(self, count, grids):
        self.count, self.lines, self.grids = count, count // PAIR, grids
        self.me = lax.axis_index("orb")
        self.row = lax.axis_index("grid")
        self.line, self.side = self.me // PAIR, self.me % PAIR
        self.partner = self.line * PAIR + (1 - self.side)

    def peer(self, step):
        return (self.line + step) % self.lines

    def at_line(self, line):
        return {"orb": line * PAIR + self.side, "grid": self.row}

    def across(self):
        return {"orb": self.partner, "grid": self.row}

    def up(self):
        return {"orb": self.me, "grid": self.row - 1}

    def down(self):
        return {"orb": self.me, "grid": self.row + 1}


def enter(ring, with_grid):
    barrier = pltpu.get_barrier_semaphore()
    pl.semaphore_signal(barrier, inc=1, device_id=ring.across(), device_id_type=MESH)
    for step in range(1, ring.lines):
        target = ring.at_line(ring.peer(step))
        pl.semaphore_signal(barrier, inc=1, device_id=target, device_id_type=MESH)
    if with_grid:

        @pl.when(ring.row > 0)
        def _():
            pl.semaphore_signal(barrier, inc=1, device_id=ring.up(), device_id_type=MESH)

        @pl.when(ring.row < ring.grids - 1)
        def _():
            pl.semaphore_signal(barrier, inc=1, device_id=ring.down(), device_id_type=MESH)

    peers = ring.lines
    if with_grid:
        last = ring.grids - 1
        peers = peers + (ring.row + last) // ring.grids + (2 * last - ring.row) // ring.grids
    pl.semaphore_wait(barrier, peers)


def piece(ref, count, index, start, rows):
    split = count // ref.shape[0]
    if split == 1:
        return ref.at[index, pl.ds(start, rows)]
    width = ref.shape[2] // split
    lane = pl.multiple_of((index % split) * width, 128)
    return ref.at[index // split, pl.ds(start, rows), pl.ds(lane, width)]


def send(src, dst, send_sem, recv_sem, target):
    return pltpu.make_async_remote_copy(
        src_ref=src, dst_ref=dst, send_sem=send_sem, recv_sem=recv_sem,
        device_id=target, device_id_type=MESH,
    )


def start_cross(ring, data, crossed, sems, rows):
    copies = []
    for step in list(range(1, ring.lines)) + [0]:
        line = ring.peer(step)
        src = piece(data, ring.count, line * PAIR + (1 - ring.side), 0, rows)
        copy = send(src, crossed.at[line], sems.at[0, line], sems.at[1, line], ring.across())
        copy.start()
        copies.append((step, copy))
    return copies


def line_scatter(ring, data, crossed, merged, gathered, copies, sems, rows, merge):
    sent = []
    for step, copy in copies:
        line = ring.peer(step)
        copy.wait_recv()
        mine = piece(data, ring.count, line * PAIR + ring.side, 0, rows)[...]
        value = merge(line * PAIR + ring.side, mine, crossed[line])
        if step == 0:
            gathered[ring.line] = value
        else:
            merged[step] = value
            out = send(
                merged.at[step], gathered.at[ring.line],
                sems.at[0, line], sems.at[1, ring.line], ring.at_line(line),
            )
            out.start()
            sent.append((line, out))
    for line, out in sent:
        send(
            merged.at[1], gathered.at[line], sems.at[0, line], sems.at[1, line], ring.at_line(line)
        ).wait_recv()
    return sent


def line_gather(ring, full, start, rows, line_sems, side_sems, arrived):
    own = piece(full, ring.count, ring.me, start, rows)
    sent = []
    for step in range(1, ring.lines):
        line = ring.peer(step)
        out = send(own, own, line_sems.at[0, line], line_sems.at[1, ring.line], ring.at_line(line))
        out.start()
        sent.append(out)
    out = send(
        own, own, side_sems.at[0, ring.line], side_sems.at[1, ring.line], ring.across()
    )
    out.start()
    sent.append(out)
    arrived(ring.me)
    for step in range(1, ring.lines):
        line = ring.peer(step)
        part = piece(full, ring.count, line * PAIR + ring.side, start, rows)
        send(part, part, line_sems.at[0, line], line_sems.at[1, line], ring.at_line(line)).wait_recv()
        out = send(part, part, side_sems.at[0, line], side_sems.at[1, line], ring.across())
        out.start()
        sent.append(out)
        arrived(line * PAIR + ring.side)
    for step in range(ring.lines):
        line = ring.peer(step)
        index = line * PAIR + (1 - ring.side)
        part = piece(full, ring.count, index, start, rows)
        send(part, part, side_sems.at[0, line], side_sems.at[1, line], ring.across()).wait_recv()
        arrived(index)
    return sent


def spread_kernel(
    count, grids, blocks, owner_ref, pot_ref, orb_ref, local_ref, trial_out, orb_out, local_out,
    crossed, merged, gathered, cross_sems, scatter_sems, line_sems, side_sems, halo_sems, edge_sems,
):
    ring = Ring(count, grids)
    rows = orb_ref.shape[1]
    last = HALO + rows
    per_block = count // blocks
    enter(ring, True)
    copies = start_cross(ring, pot_ref, crossed, cross_sems, rows)
    has_up, has_down = ring.row > 0, ring.row < grids - 1

    def edge_up(make):
        return [
            make(orb_ref.at[:, pl.ds(0, HALO)], orb_out.at[:, pl.ds(last, HALO)], 0),
            make(local_ref.at[pl.ds(0, HALO)], local_out.at[pl.ds(last, HALO)], 1),
        ]

    def edge_down(make):
        return [
            make(orb_ref.at[:, pl.ds(rows - HALO, HALO)], orb_out.at[:, pl.ds(0, HALO)], 2),
            make(local_ref.at[pl.ds(rows - HALO, HALO)], local_out.at[pl.ds(0, HALO)], 3),
        ]

    def edge(target):
        return lambda src, dst, k: send(src, dst, edge_sems.at[0, k], edge_sems.at[1, k], target)

    @pl.when(has_up)
    def _():
        for copy in edge_up(edge(ring.up())):
            copy.start()

    @pl.when(has_down)
    def _():
        for copy in edge_down(edge(ring.down())):
            copy.start()

    orb_out[:, HALO:last] = orb_ref[...]
    local_out[HALO:last] = local_ref[...]

    @pl.when(jnp.logical_not(has_up))
    def _():
        orb_out[:, 0:HALO] = jnp.zeros((orb_ref.shape[0], HALO, orb_ref.shape[2]), jnp.float32)
        local_out[0:HALO] = jnp.zeros((HALO, orb_ref.shape[2]), jnp.float32)
        trial_out[:, 0:HALO] = jnp.zeros((pot_ref.shape[0], HALO, orb_ref.shape[2]), jnp.float32)

    @pl.when(jnp.logical_not(has_down))
    def _():
        orb_out[:, last:] = jnp.zeros((orb_ref.shape[0], HALO, orb_ref.shape[2]), jnp.float32)
        local_out[last:] = jnp.zeros((HALO, orb_ref.shape[2]), jnp.float32)
        trial_out[:, last:] = jnp.zeros((pot_ref.shape[0], HALO, orb_ref.shape[2]), jnp.float32)

    def choose(index, mine, other):
        return jnp.where(owner_ref[index // per_block] == ring.partner, other, mine)

    sent = line_scatter(
        ring, pot_ref, crossed, merged, gathered, copies, scatter_sems, rows, choose
    )
    piece(trial_out, count, ring.me, HALO, rows)[...] = gathered[
        owner_ref[ring.me // per_block] // PAIR
    ]

    def halo_up(index):
        return send(
            piece(trial_out, count, index, HALO, HALO), piece(trial_out, count, index, last, HALO),
            halo_sems.at[0, 0, index], halo_sems.at[1, 0, index], ring.up(),
        )

    def halo_down(index):
        return send(
            piece(trial_out, count, index, rows, HALO), piece(trial_out, count, index, 0, HALO),
            halo_sems.at[0, 1, index], halo_sems.at[1, 1, index], ring.down(),
        )

    def arrived(index):
        @pl.when(has_up)
        def _():
            halo_up(index).start()

        @pl.when(has_down)
        def _():
            halo_down(index).start()

    more = line_gather(ring, trial_out, HALO, rows, line_sems, side_sems, arrived)

    @pl.when(has_up)
    def _():
        for copy in edge_up(edge(ring.up())):
            copy.wait_send()
        for copy in edge_down(edge(ring.up())):
            copy.wait_recv()
        for index in range(count):
            halo_up(index).wait_send()
            halo_down(index).wait_recv()

    @pl.when(has_down)
    def _():
        for copy in edge_down(edge(ring.down())):
            copy.wait_send()
        for copy in edge_up(edge(ring.down())):
            copy.wait_recv()
        for index in range(count):
            halo_down(index).wait_send()
            halo_up(index).wait_recv()

    for step, copy in copies:
        copy.wait_send()
    for line, copy in sent:
        copy.wait_send()
    for copy in more:
        copy.wait_send()


def total_kernel(
    count, grids, part_ref, out_ref,
    crossed, merged, gathered, cross_sems, scatter_sems, line_sems, side_sems,
):
    ring = Ring(count, grids)
    rows = part_ref.shape[1]
    enter(ring, False)
    copies = start_cross(ring, part_ref, crossed, cross_sems, rows)
    sent = line_scatter(
        ring, part_ref, crossed, merged, gathered, copies, scatter_sems, rows,
        lambda index, mine, other: mine + other,
    )
    total = gathered[0]
    for line in range(1, ring.lines):
        total = total + gathered[line]
    piece(out_ref, count, ring.me, 0, rows)[...] = total
    more = line_gather(ring, out_ref, 0, rows, line_sems, side_sems, lambda index: None)
    for step, copy in copies:
        copy.wait_send()
    for line, copy in sent:
        copy.wait_send()
    for copy in more:
        copy.wait_send()


def band_matrix(depth, width):
    k = lax.broadcasted_iota(jnp.int32, (depth, width), 0)
    n = lax.broadcasted_iota(jnp.int32, (depth, width), 1) + width // 2
    far_y, far_z = jnp.abs(k // NZ - n // NZ), jnp.abs(k % NZ - n % NZ)
    near = ((far_y == 1) & (far_z == 0)) | ((far_y == 0) & (far_z == 1))
    far = ((far_y == 2) & (far_z == 0)) | ((far_y == 0) & (far_z == 2))
    return jnp.where(near, 16.0, jnp.where(far, -1.0, 0.0)).astype(jnp.bfloat16)


WIDTH = 256


def sweep_kernel(
    grids, shift_ref, weight_ref, trial_ref, orb_ref, local_ref, out_ref,
    trials, first, scale, now_a, now_b, hi_a, hi_b, lo_a, lo_b, product, density, band, inverse,
):
    n = pl.program_id(0)
    batch, planes, cells = trial_ref.shape
    rows = planes - 2 * HALO

    @pl.when(n == 0)
    def _():
        band[...] = band_matrix(2 * WIDTH, WIDTH)
        density[...] = jnp.zeros_like(density)
        for x in range(planes):
            trials[x] = trial_ref[:, x, :]

    place = lax.axis_index("grid") * rows - HALO
    where = lax.broadcasted_iota(jnp.int32, (planes, cells), 0) + place
    inside = (where >= 0) & (where < rows * grids)
    diagonal = KINETIC_DIAG + (local_ref[...] + shift_ref[n])
    inverse[...] = jnp.where(inside, 1.0 / diagonal, 0.0)

    def split(value):
        high = value.astype(jnp.bfloat16)
        return high, (value - high.astype(jnp.float32)).astype(jnp.bfloat16)

    for x in range(0, planes, 2):
        values = []
        for p in (x, x + 1):
            inv = jnp.broadcast_to(inverse[pl.ds(p, 1), :], (batch, cells))
            orb = jnp.broadcast_to(orb_ref[n, pl.ds(p, 1), :], (batch, cells))
            scale[p] = inv * (1.0 / 24.0)
            value = -(trials[p] * orb) * inv
            first[p] = value
            values.append(value)
        high, low = split(jnp.concatenate(values, axis=0))
        hi_a[x * batch : (x + 2) * batch] = high
        lo_a[x * batch : (x + 2) * batch] = low

    weight = weight_ref[n].astype(jnp.float32)
    current = first
    buffers = ((now_a, hi_a, lo_a), (now_b, hi_b, lo_b))
    for repeat in range(ITERS):
        hi_in, lo_in = buffers[repeat % 2][1:]
        target, hi_out, lo_out = buffers[(repeat + 1) % 2]
        margin = REACH * (repeat + 1)
        extent = planes - 2 * margin
        for left in range(0, cells, WIDTH):
            a = max(0, left - WIDTH // 2)
            b = min(cells, left + WIDTH + WIDTH // 2)
            k = a - (left - WIDTH // 2)
            weights = band[k : k + b - a, :]
            span = slice(margin * batch, (margin + extent) * batch)
            product[0 : extent * batch] = jnp.dot(
                hi_in[span, a:b], weights, preferred_element_type=jnp.float32
            ) + jnp.dot(lo_in[span, a:b], weights, preferred_element_type=jnp.float32)
            lanes = slice(left, left + WIDTH)
            for x in range(margin, margin + extent, 2):
                values = []
                for p in (x, x + 1):
                    near = current[p - 1, :, lanes] + current[p + 1, :, lanes]
                    far = current[p - 2, :, lanes] + current[p + 2, :, lanes]
                    spot = (p - margin) * batch
                    moved = product[spot : spot + batch] + (16.0 * near - far)
                    value = first[p, :, lanes] + scale[p, :, lanes] * moved
                    if repeat == ITERS - 1:
                        orb = weight * orb_ref[n, pl.ds(p, 1), lanes]
                        density[p - margin, :, lanes] += orb * value
                    else:
                        target[p, :, lanes] = value
                        values.append(value)
                if values:
                    high, low = split(jnp.concatenate(values, axis=0))
                    hi_out[x * batch : (x + 2) * batch, lanes] = high
                    lo_out[x * batch : (x + 2) * batch, lanes] = low
        current = target

    @pl.when(n == pl.num_programs(0) - 1)
    def _():
        for x in range(rows):
            out_ref[:, x, :] = density[x]


def shards(count, grids, potentials, orbitals, local_pot, shifts, occupation, owner):
    _, blocks, kinds, rows, cells = potentials.shape
    batch = blocks * kinds
    orbital_count = orbitals.shape[0]
    lines = count // PAIR
    planes = rows + 2 * HALO
    stored = potentials.reshape(batch, rows, cells)
    part = (rows, cells * batch // count)
    vmem = pl.BlockSpec(memory_space=pltpu.VMEM)
    smem = pl.BlockSpec(memory_space=pltpu.SMEM)
    f32 = jnp.float32
    dma = pltpu.SemaphoreType.DMA
    moving = [
        pltpu.VMEM((lines,) + part, f32),
        pltpu.VMEM((lines,) + part, f32),
        pltpu.VMEM((lines,) + part, f32),
        dma((2, lines)), dma((2, lines)), dma((2, lines)), dma((2, lines)),
    ]
    trials, orbs, local = pl.pallas_call(
        functools.partial(spread_kernel, count, grids, blocks),
        out_shape=[
            jax.ShapeDtypeStruct((batch, planes, cells), f32),
            jax.ShapeDtypeStruct((orbital_count, planes, cells), f32),
            jax.ShapeDtypeStruct((planes, cells), f32),
        ],
        in_specs=[smem, vmem, vmem, vmem],
        out_specs=[vmem] * 3,
        scratch_shapes=moving + [dma((2, 2, count)), dma((2, 4))],
        compiler_params=pltpu.CompilerParams(collective_id=0, has_side_effects=True),
        name="spread",
    )(owner, stored, orbitals, local_pot)

    big = pltpu.VMEM((planes, batch, cells), f32)
    half = pltpu.VMEM((planes * batch, cells), jnp.bfloat16)
    partial = pl.pallas_call(
        functools.partial(sweep_kernel, grids),
        out_shape=jax.ShapeDtypeStruct((batch, rows, cells), f32),
        grid=(orbital_count,),
        in_specs=[smem, smem, vmem, vmem, vmem],
        out_specs=vmem,
        scratch_shapes=[big, big, big, big, big, half, half, half, half]
        + [
            pltpu.VMEM((planes * batch, WIDTH), f32),
            pltpu.VMEM((rows, batch, cells), f32),
            pltpu.VMEM((2 * WIDTH, WIDTH), jnp.bfloat16),
            pltpu.VMEM((planes, cells), f32),
        ],
        compiler_params=pltpu.CompilerParams(dimension_semantics=("arbitrary",)),
        name="sweeps",
    )(shifts, occupation, trials, orbs, local)

    totals = pl.pallas_call(
        functools.partial(total_kernel, count, grids),
        out_shape=jax.ShapeDtypeStruct((batch, rows, cells), f32),
        in_specs=[vmem],
        out_specs=vmem,
        scratch_shapes=moving,
        compiler_params=pltpu.CompilerParams(collective_id=1, has_side_effects=True),
        name="total",
    )(partial)
    owned = (owner == lax.axis_index("orb"))[:, None, None, None]
    return jnp.where(owned, totals.reshape(blocks, kinds, rows, cells), 0.0)[None]


def solution(mesh):
    in_specs = (
        P("orb", None, None, "grid", None),
        P("orb", "grid", None),
        P("grid", None),
        P("orb"),
        P("orb"),
        P(),
    )
    out_specs = P("orb", None, None, "grid", None)
    body = functools.partial(shards, mesh.shape["orb"], mesh.shape["grid"])
    return jax.shard_map(body, mesh=mesh, in_specs=in_specs, out_specs=out_specs, check_vma=False)
```

```python
import functools

import jax
import jax.numpy as jnp
from jax import lax
from jax.experimental import pallas as pl
from jax.experimental.pallas import tpu as pltpu
from jax.sharding import PartitionSpec as P

NZ = 32
ITERS = 4
REACH = 2
HALO = REACH * ITERS
KINETIC_DIAG = 3.75
PAIR = 2
MESH = pl.DeviceIdType.MESH


class Ring:
    def __init__(self, count, grids):
        self.count, self.lines, self.grids = count, count // PAIR, grids
        self.me = lax.axis_index("orb")
        self.row = lax.axis_index("grid")
        self.line, self.side = self.me // PAIR, self.me % PAIR
        self.partner = self.line * PAIR + (1 - self.side)

    def peer(self, step):
        return (self.line + step) % self.lines

    def at_line(self, line):
        return {"orb": line * PAIR + self.side, "grid": self.row}

    def across(self):
        return {"orb": self.partner, "grid": self.row}

    def up(self):
        return {"orb": self.me, "grid": self.row - 1}

    def down(self):
        return {"orb": self.me, "grid": self.row + 1}


def enter(ring, with_grid):
    barrier = pltpu.get_barrier_semaphore()
    pl.semaphore_signal(barrier, inc=1, device_id=ring.across(), device_id_type=MESH)
    for step in range(1, ring.lines):
        target = ring.at_line(ring.peer(step))
        pl.semaphore_signal(barrier, inc=1, device_id=target, device_id_type=MESH)
    if with_grid:

        @pl.when(ring.row > 0)
        def _():
            pl.semaphore_signal(barrier, inc=1, device_id=ring.up(), device_id_type=MESH)

        @pl.when(ring.row < ring.grids - 1)
        def _():
            pl.semaphore_signal(barrier, inc=1, device_id=ring.down(), device_id_type=MESH)

    peers = ring.lines
    if with_grid:
        last = ring.grids - 1
        peers = peers + (ring.row + last) // ring.grids + (2 * last - ring.row) // ring.grids
    pl.semaphore_wait(barrier, peers)


def piece(ref, count, index, start, rows):
    split = count // ref.shape[0]
    if split == 1:
        return ref.at[index, pl.ds(start, rows)]
    width = ref.shape[2] // split
    lane = pl.multiple_of((index % split) * width, 128)
    return ref.at[index // split, pl.ds(start, rows), pl.ds(lane, width)]


def send(src, dst, send_sem, recv_sem, target):
    return pltpu.make_async_remote_copy(
        src_ref=src, dst_ref=dst, send_sem=send_sem, recv_sem=recv_sem,
        device_id=target, device_id_type=MESH,
    )


def start_cross(ring, data, crossed, sems, rows):
    copies = []
    for step in list(range(1, ring.lines)) + [0]:
        line = ring.peer(step)
        src = piece(data.at[1 - ring.side], ring.lines, line, 0, rows)
        copy = send(src, crossed.at[line], sems.at[0, line], sems.at[1, line], ring.across())
        copy.start()
        copies.append((step, copy))
    return copies


def line_gather(ring, full, start, rows, sems, arrived):
    own = piece(full, ring.lines, ring.line, start, rows)
    sent = []
    for step in range(1, ring.lines):
        line = ring.peer(step)
        out = send(own, own, sems.at[0, line], sems.at[1, ring.line], ring.at_line(line))
        out.start()
        sent.append(out)
    sent += arrived(ring.line)
    for step in range(1, ring.lines):
        line = ring.peer(ring.lines - step)
        part = piece(full, ring.lines, line, start, rows)
        send(part, part, sems.at[0, line], sems.at[1, line], ring.at_line(line)).wait_recv()
        sent += arrived(line)
    return sent


def spread_kernel(
    count, grids, kinds, owner_ref, shift_ref, weight_ref, pot_ref, orb_ref, local_ref,
    trial_out, orb_out, local_out, pack_out,
    crossed, merged, gathered, cross_sems, scatter_sems, line_sems, halo_sems, edge_sems, pair_sems,
):
    ring = Ring(count, grids)
    orbitals, rows, cells = orb_ref.shape
    half = pot_ref.shape[1]
    split = ring.lines // half
    last = HALO + rows
    has_up, has_down = ring.row > 0, ring.row < grids - 1
    for n in range(orbitals):
        pack_out[0, n] = jnp.full((cells,), shift_ref[n], jnp.float32)
        pack_out[0, orbitals + n] = jnp.full((cells,), weight_ref[n].astype(jnp.float32), jnp.float32)
    enter(ring, True)
    copies = start_cross(ring, pot_ref, crossed, cross_sems, rows)
    center = send(
        orb_ref, orb_out.at[1, :, pl.ds(HALO, rows)],
        pair_sems.at[0, 0], pair_sems.at[1, 0], ring.across(),
    )
    center.start()
    pack = send(
        pack_out.at[0], pack_out.at[1], pair_sems.at[0, 1], pair_sems.at[1, 1], ring.across()
    )
    pack.start()

    def edge_up(target):
        def make(src, dst, k):
            return send(src, dst, edge_sems.at[0, k], edge_sems.at[1, k], target)

        return [
            make(orb_ref.at[:, pl.ds(0, HALO)], orb_out.at[0, :, pl.ds(last, HALO)], 0),
            make(local_ref.at[pl.ds(0, HALO)], local_out.at[pl.ds(last, HALO)], 1),
            make(orb_out.at[1, :, pl.ds(HALO, HALO)], orb_out.at[1, :, pl.ds(last, HALO)], 2),
        ]

    def edge_down(target):
        def make(src, dst, k):
            return send(src, dst, edge_sems.at[0, k], edge_sems.at[1, k], target)

        return [
            make(orb_ref.at[:, pl.ds(rows - HALO, HALO)], orb_out.at[0, :, pl.ds(0, HALO)], 3),
            make(local_ref.at[pl.ds(rows - HALO, HALO)], local_out.at[pl.ds(0, HALO)], 4),
            make(orb_out.at[1, :, pl.ds(rows, HALO)], orb_out.at[1, :, pl.ds(0, HALO)], 5),
        ]

    @pl.when(has_up)
    def _():
        for copy in edge_up(ring.up())[:2]:
            copy.start()

    @pl.when(has_down)
    def _():
        for copy in edge_down(ring.down())[:2]:
            copy.start()

    orb_out[0, :, HALO:last] = orb_ref[...]
    local_out[HALO:last] = local_ref[...]

    def clear(start):
        orb_out[:, :, start : start + HALO] = jnp.zeros((2, orbitals, HALO, cells), jnp.float32)
        local_out[start : start + HALO] = jnp.zeros((HALO, cells), jnp.float32)
        trial_out[:, start : start + HALO] = jnp.zeros((half, HALO, cells), jnp.float32)

    @pl.when(jnp.logical_not(has_up))
    def _():
        clear(0)

    @pl.when(jnp.logical_not(has_down))
    def _():
        clear(last)

    def owner_of(line):
        return owner_ref[(ring.side * half + line // split) // kinds]

    sent = []
    for step, copy in copies:
        line = ring.peer(step)
        copy.wait_recv()
        mine = piece(pot_ref.at[ring.side], ring.lines, line, 0, rows)[...]
        value = jnp.where(owner_of(line) == ring.partner, crossed[line], mine)
        if step == 0:
            gathered[ring.line] = value
        else:
            merged[step] = value
            out = send(
                merged.at[step], gathered.at[ring.line],
                scatter_sems.at[0, line], scatter_sems.at[1, ring.line], ring.at_line(line),
            )
            out.start()
            sent.append(out)
    for step in range(1, ring.lines):
        line = ring.peer(step)
        send(
            merged.at[step], gathered.at[line],
            scatter_sems.at[0, line], scatter_sems.at[1, line], ring.at_line(line),
        ).wait_recv()
    piece(trial_out, ring.lines, ring.line, HALO, rows)[...] = gathered[owner_of(ring.line) // PAIR]

    def halo_up(index):
        return send(
            piece(trial_out, ring.lines, index, HALO, HALO),
            piece(trial_out, ring.lines, index, last, HALO),
            halo_sems.at[0, 0, index], halo_sems.at[1, 0, index], ring.up(),
        )

    def halo_down(index):
        return send(
            piece(trial_out, ring.lines, index, rows, HALO),
            piece(trial_out, ring.lines, index, 0, HALO),
            halo_sems.at[0, 1, index], halo_sems.at[1, 1, index], ring.down(),
        )

    def arrived(index):
        @pl.when(has_up)
        def _():
            halo_up(index).start()

        @pl.when(has_down)
        def _():
            halo_down(index).start()

        return []

    def arrived_first(index):
        arrived(index)
        center.wait_recv()

        @pl.when(has_up)
        def _():
            edge_up(ring.up())[2].start()

        @pl.when(has_down)
        def _():
            edge_down(ring.down())[2].start()

        return []

    calls = [arrived_first] + [arrived] * (ring.lines - 1)
    sent += line_gather(
        ring, trial_out, HALO, rows, line_sems, lambda index: calls.pop(0)(index)
    )

    @pl.when(has_up)
    def _():
        for copy in edge_up(ring.up()):
            copy.wait_send()
        for copy in edge_down(ring.up()):
            copy.wait_recv()
        for index in range(ring.lines):
            halo_up(index).wait_send()
            halo_down(index).wait_recv()

    @pl.when(has_down)
    def _():
        for copy in edge_down(ring.down()):
            copy.wait_send()
        for copy in edge_up(ring.down()):
            copy.wait_recv()
        for index in range(ring.lines):
            halo_down(index).wait_send()
            halo_up(index).wait_recv()

    pack.wait_recv()
    for copy in [copy for step, copy in copies] + sent + [center, pack]:
        copy.wait_send()


def total_kernel(count, grids, part_ref, out_ref, gathered, scatter_sems, line_sems, side_sems):
    ring = Ring(count, grids)
    rows = part_ref.shape[1]
    enter(ring, False)
    sent = []
    for step in range(1, ring.lines):
        line = ring.peer(step)
        out = send(
            piece(part_ref, ring.lines, line, 0, rows), gathered.at[ring.line],
            scatter_sems.at[0, line], scatter_sems.at[1, ring.line], ring.at_line(line),
        )
        out.start()
        sent.append(out)
    own = piece(part_ref, ring.lines, ring.line, 0, rows)
    total = own[...]
    for step in range(1, ring.lines):
        line = ring.peer(ring.lines - step)
        send(
            own, gathered.at[line],
            scatter_sems.at[0, line], scatter_sems.at[1, line], ring.at_line(line),
        ).wait_recv()
        total = total + gathered[line]
    mine, other = out_ref.at[ring.side], out_ref.at[1 - ring.side]
    piece(mine, ring.lines, ring.line, 0, rows)[...] = total

    def arrived(line):
        part = piece(mine, ring.lines, line, 0, rows)
        out = send(part, part, side_sems.at[0, line], side_sems.at[1, line], ring.across())
        out.start()
        return [out]

    sent += line_gather(ring, mine, 0, rows, line_sems, arrived)
    for step in range(ring.lines):
        line = ring.peer(ring.lines - step)
        part = piece(other, ring.lines, line, 0, rows)
        send(part, part, side_sems.at[0, line], side_sems.at[1, line], ring.across()).wait_recv()
    for copy in sent:
        copy.wait_send()


def band_matrix(depth, width):
    k = lax.broadcasted_iota(jnp.int32, (depth, width), 0)
    n = lax.broadcasted_iota(jnp.int32, (depth, width), 1) + width // 2
    far_y, far_z = jnp.abs(k // NZ - n // NZ), jnp.abs(k % NZ - n % NZ)
    near = ((far_y == 1) & (far_z == 0)) | ((far_y == 0) & (far_z == 1))
    far = ((far_y == 2) & (far_z == 0)) | ((far_y == 0) & (far_z == 2))
    return jnp.where(near, 16.0, jnp.where(far, -1.0, 0.0)).astype(jnp.bfloat16)


WIDTH = 256


def sweep_kernel(
    grids, pack_ref, trial_ref, orb_ref, local_ref, out_ref,
    trials, first, scale, now_a, now_b, hi_a, hi_b, lo_a, lo_b, product, density, band, inverse,
    weighted,
):
    n = pl.program_id(0)
    half, planes, cells = trial_ref.shape
    orbitals = orb_ref.shape[1]
    batch = PAIR * half
    rows = planes - 2 * HALO

    @pl.when(n == 0)
    def _():
        band[...] = band_matrix(2 * WIDTH, WIDTH)
        density[...] = jnp.zeros_like(density)
        for x in range(planes):
            trials[x] = jnp.concatenate([trial_ref[:, x, :]] * PAIR, axis=0)

    place = lax.axis_index("grid") * rows - HALO
    where = lax.broadcasted_iota(jnp.int32, (planes, cells), 0) + place
    inside = (where >= 0) & (where < rows * grids)
    for k in range(PAIR):
        diagonal = KINETIC_DIAG + (local_ref[...] + pack_ref[k, pl.ds(n, 1), :])
        inverse[k] = jnp.where(inside, 1.0 / diagonal, 0.0)

    lower = lax.broadcasted_iota(jnp.int32, (batch, cells), 0) < half

    def both(a, b):
        return jnp.where(
            lower, jnp.broadcast_to(a, (batch, cells)), jnp.broadcast_to(b, (batch, cells))
        )

    def split(value):
        high = value.astype(jnp.bfloat16)
        return high, (value - high.astype(jnp.float32)).astype(jnp.bfloat16)

    weight = both(pack_ref[0, pl.ds(orbitals + n, 1), :], pack_ref[1, pl.ds(orbitals + n, 1), :])
    for x in range(0, planes, 2):
        values = []
        for p in (x, x + 1):
            inv = both(inverse[0, pl.ds(p, 1), :], inverse[1, pl.ds(p, 1), :])
            orb = both(orb_ref[0, n, pl.ds(p, 1), :], orb_ref[1, n, pl.ds(p, 1), :])
            scale[p] = inv * (1.0 / 24.0)
            value = -(trials[p] * orb) * inv
            first[p] = value
            values.append(value)
            if HALO <= p < HALO + rows:
                weighted[p - HALO] = weight * orb
        high, low = split(jnp.concatenate(values, axis=0))
        hi_a[x * batch : (x + 2) * batch] = high
        lo_a[x * batch : (x + 2) * batch] = low

    current = first
    buffers = ((now_a, hi_a, lo_a), (now_b, hi_b, lo_b))
    for repeat in range(ITERS):
        hi_in, lo_in = buffers[repeat % 2][1:]
        target, hi_out, lo_out = buffers[(repeat + 1) % 2]
        margin = REACH * (repeat + 1)
        extent = planes - 2 * margin
        for left in range(0, cells, WIDTH):
            a = max(0, left - WIDTH // 2)
            b = min(cells, left + WIDTH + WIDTH // 2)
            k = a - (left - WIDTH // 2)
            weights = band[k : k + b - a, :]
            span = slice(margin * batch, (margin + extent) * batch)
            product[0 : extent * batch] = jnp.dot(
                hi_in[span, a:b], weights, preferred_element_type=jnp.float32
            ) + jnp.dot(lo_in[span, a:b], weights, preferred_element_type=jnp.float32)
            lanes = slice(left, left + WIDTH)
            for x in range(margin, margin + extent, 2):
                values = []
                for p in (x, x + 1):
                    near = current[p - 1, :, lanes] + current[p + 1, :, lanes]
                    far = current[p - 2, :, lanes] + current[p + 2, :, lanes]
                    spot = (p - margin) * batch
                    moved = product[spot : spot + batch] + (16.0 * near - far)
                    value = first[p, :, lanes] + scale[p, :, lanes] * moved
                    if repeat == ITERS - 1:
                        density[p - margin, :, lanes] += weighted[p - margin, :, lanes] * value
                    else:
                        target[p, :, lanes] = value
                        values.append(value)
                if values:
                    high, low = split(jnp.concatenate(values, axis=0))
                    hi_out[x * batch : (x + 2) * batch, lanes] = high
                    lo_out[x * batch : (x + 2) * batch, lanes] = low
        current = target

    @pl.when(n == pl.num_programs(0) - 1)
    def _():
        for x in range(rows):
            out_ref[:, x, :] = density[x, 0:half] + density[x, half:batch]


def shards(count, grids, potentials, orbitals, local_pot, shifts, occupation, owner):
    _, blocks, kinds, rows, cells = potentials.shape
    batch = blocks * kinds
    half = batch // PAIR
    orbital_count = orbitals.shape[0]
    lines = count // PAIR
    planes = rows + 2 * HALO
    stored = potentials.reshape(PAIR, half, rows, cells)
    vmem = pl.BlockSpec(memory_space=pltpu.VMEM)
    smem = pl.BlockSpec(memory_space=pltpu.SMEM)
    f32 = jnp.float32
    dma = pltpu.SemaphoreType.DMA
    slots = pltpu.VMEM((lines, rows, cells * half // lines), f32)
    trials, orbs, local, pack = pl.pallas_call(
        functools.partial(spread_kernel, count, grids, kinds),
        out_shape=[
            jax.ShapeDtypeStruct((half, planes, cells), f32),
            jax.ShapeDtypeStruct((PAIR, orbital_count, planes, cells), f32),
            jax.ShapeDtypeStruct((planes, cells), f32),
            jax.ShapeDtypeStruct((PAIR, 2 * orbital_count, cells), f32),
        ],
        in_specs=[smem, smem, smem, vmem, vmem, vmem],
        out_specs=[vmem] * 4,
        scratch_shapes=[
            slots, slots, slots,
            dma((2, lines)), dma((2, lines)), dma((2, lines)),
            dma((2, 2, lines)), dma((2, 6)), dma((2, 2)),
        ],
        compiler_params=pltpu.CompilerParams(collective_id=0, has_side_effects=True),
        name="spread",
    )(owner, shifts, occupation, stored, orbitals, local_pot)

    big = pltpu.VMEM((planes, batch, cells), f32)
    packed = pltpu.VMEM((planes * batch, cells), jnp.bfloat16)
    partial = pl.pallas_call(
        functools.partial(sweep_kernel, grids),
        out_shape=jax.ShapeDtypeStruct((half, rows, cells), f32),
        grid=(orbital_count,),
        in_specs=[vmem] * 4,
        out_specs=vmem,
        scratch_shapes=[big, big, big, big, big, packed, packed, packed, packed]
        + [
            pltpu.VMEM((planes * batch, WIDTH), f32),
            pltpu.VMEM((rows, batch, cells), f32),
            pltpu.VMEM((2 * WIDTH, WIDTH), jnp.bfloat16),
            pltpu.VMEM((PAIR, planes, cells), f32),
            pltpu.VMEM((rows, batch, cells), f32),
        ],
        compiler_params=pltpu.CompilerParams(dimension_semantics=("arbitrary",)),
        name="sweeps",
    )(pack, trials, orbs, local)

    totals = pl.pallas_call(
        functools.partial(total_kernel, count, grids),
        out_shape=jax.ShapeDtypeStruct((PAIR, half, rows, cells), f32),
        in_specs=[vmem],
        out_specs=vmem,
        scratch_shapes=[slots, dma((2, lines)), dma((2, lines)), dma((2, lines))],
        compiler_params=pltpu.CompilerParams(collective_id=1, has_side_effects=True),
        name="total",
    )(partial)
    owned = (owner == lax.axis_index("orb"))[:, None, None, None]
    return jnp.where(owned, totals.reshape(blocks, kinds, rows, cells), 0.0)[None]


def solution(mesh):
    in_specs = (
        P("orb", None, None, "grid", None),
        P("orb", "grid", None),
        P("grid", None),
        P("orb"),
        P("orb"),
        P(),
    )
    out_specs = P("orb", None, None, "grid", None)
    body = functools.partial(shards, mesh.shape["orb"], mesh.shape["grid"])
    return jax.shard_map(body, mesh=mesh, in_specs=in_specs, out_specs=out_specs, check_vma=False)
```

```python
import functools

import jax
import jax.numpy as jnp
from jax import lax
from jax.experimental import pallas as pl
from jax.experimental.pallas import tpu as pltpu
from jax.sharding import PartitionSpec as P

NZ = 32
ITERS = 4
REACH = 2
HALO = REACH * ITERS
KINETIC_DIAG = 3.75
PAIR = 2
MESH = pl.DeviceIdType.MESH


class Ring:
    def __init__(self, count, grids):
        self.count, self.lines, self.grids = count, count // PAIR, grids
        self.me = lax.axis_index("orb")
        self.row = lax.axis_index("grid")
        self.line, self.side = self.me // PAIR, self.me % PAIR
        self.partner = self.line * PAIR + (1 - self.side)

    def at_line(self, line):
        return {"orb": line * PAIR + self.side, "grid": self.row}

    def across(self):
        return {"orb": self.partner, "grid": self.row}

    def up(self):
        return {"orb": self.me, "grid": self.row - 1}

    def down(self):
        return {"orb": self.me, "grid": self.row + 1}


def enter(ring, with_grid):
    barrier = pltpu.get_barrier_semaphore()
    top = ring.lines - 1

    def greet(target):
        pl.semaphore_signal(barrier, inc=1, device_id=target, device_id_type=MESH)

    greet(ring.across())

    @pl.when(ring.line > 0)
    def _():
        greet(ring.at_line(ring.line - 1))

    @pl.when(ring.line < top)
    def _():
        greet(ring.at_line(ring.line + 1))

    peers = 1 + (ring.line + top) // ring.lines + (2 * top - ring.line) // ring.lines
    if with_grid:

        @pl.when(ring.row > 0)
        def _():
            greet(ring.up())

        @pl.when(ring.row < ring.grids - 1)
        def _():
            greet(ring.down())

        last = ring.grids - 1
        peers = peers + (ring.row + last) // ring.grids + (2 * last - ring.row) // ring.grids
    pl.semaphore_wait(barrier, peers)


def send(src, dst, send_sem, recv_sem, target):
    return pltpu.make_async_remote_copy(
        src_ref=src, dst_ref=dst, send_sem=send_sem, recv_sem=recv_sem,
        device_id=target, device_id_type=MESH,
    )


LAG = 2


class Waves:
    def __init__(self, ring, chunks, buffers, sems):
        self.ring, self.chunks, self.sems = ring, chunks, sems
        self.from_left, self.from_right, self.to_right, self.to_left = buffers
        self.has_left, self.has_right = ring.line > 0, ring.line < ring.lines - 1

    def right(self, q, target):
        sems = self.sems
        return send(self.to_right.at[q], self.from_left.at[q], sems.at[0, q], sems.at[1, q], target)

    def left(self, q, target):
        sems = self.sems
        return send(self.to_left.at[q], self.from_right.at[q], sems.at[2, q], sems.at[3, q], target)

    def clear(self):
        @pl.when(jnp.logical_not(self.has_left))
        def _():
            self.from_left[...] = jnp.zeros_like(self.from_left)

        @pl.when(jnp.logical_not(self.has_right))
        def _():
            self.from_right[...] = jnp.zeros_like(self.from_right)

    def run(self, prepare, onward, finish):
        ring, line, top = self.ring, self.ring.line, self.ring.lines - 1
        beyond = (2 * line) // ring.lines
        late = beyond * line + (1 - beyond) * (top - line)

        def step(s, carry):
            def event(offset, act):
                q = s - offset

                @pl.when((q >= 0) & (q < self.chunks))
                def _():
                    act(q)

            def rightward(q):
                @pl.when(self.has_left)
                def _():
                    self.right(q, ring.across()).wait_recv()

                @pl.when(self.has_right)
                def _():
                    self.to_right[q] = onward(q, self.from_left[q])
                    self.right(q, ring.at_line(line + 1)).start()

            def leftward(q):
                @pl.when(self.has_right)
                def _():
                    self.left(q, ring.across()).wait_recv()

                @pl.when(self.has_left)
                def _():
                    self.to_left[q] = onward(q, self.from_right[q])
                    self.left(q, ring.at_line(line - 1)).start()

            event(0, prepare)
            event(line * LAG, rightward)
            event((top - line) * LAG, leftward)
            event(late * LAG, finish)
            return carry

        lax.fori_loop(0, self.chunks + top * LAG, step, 0)

    def drain(self):
        @pl.when(self.has_right)
        def _():
            for q in range(self.chunks):
                self.right(q, self.ring.across()).wait_send()

        @pl.when(self.has_left)
        def _():
            for q in range(self.chunks):
                self.left(q, self.ring.across()).wait_send()


def chunk_of(ref, q, per, start=0):
    return ref.at[q // per, pl.ds(pl.multiple_of(start + (q % per) * HALO, HALO), HALO)]


def spread_kernel(
    count, grids, kinds, owner_ref, shift_ref, weight_ref, pot_ref, orb_ref, local_ref,
    trial_out, orb_out, local_out, pack_out,
    crossed, merged, from_left, from_right, to_right, to_left,
    cross_sems, wave_sems, halo_sems, edge_sems, pair_sems,
):
    ring = Ring(count, grids)
    orbitals, rows, cells = orb_ref.shape
    half = pot_ref.shape[1]
    per = rows // HALO
    chunks = half * per
    last = HALO + rows
    has_up, has_down = ring.row > 0, ring.row < grids - 1
    waves = Waves(ring, chunks, (from_left, from_right, to_right, to_left), wave_sems)
    for n in range(orbitals):
        pack_out[0, n] = jnp.full((cells,), shift_ref[n], jnp.float32)
        pack_out[0, orbitals + n] = jnp.full((cells,), weight_ref[n].astype(jnp.float32), jnp.float32)
    enter(ring, True)

    def cross(q):
        return send(
            chunk_of(pot_ref.at[1 - ring.side], q, per), crossed.at[q],
            cross_sems.at[0, q], cross_sems.at[1, q], ring.across(),
        )

    for q in range(chunks):
        cross(q).start()
    center = send(
        orb_ref, orb_out.at[1, :, pl.ds(HALO, rows)],
        pair_sems.at[0, 0], pair_sems.at[1, 0], ring.across(),
    )
    center.start()
    pack = send(
        pack_out.at[0], pack_out.at[1], pair_sems.at[0, 1], pair_sems.at[1, 1], ring.across()
    )
    pack.start()

    def edge_up(k, target):
        src, dst = [
            (orb_ref.at[:, pl.ds(0, HALO)], orb_out.at[0, :, pl.ds(last, HALO)]),
            (local_ref.at[pl.ds(0, HALO)], local_out.at[pl.ds(last, HALO)]),
            (orb_out.at[1, :, pl.ds(HALO, HALO)], orb_out.at[1, :, pl.ds(last, HALO)]),
        ][k]
        return send(src, dst, edge_sems.at[0, k], edge_sems.at[1, k], target)

    def edge_down(k, target):
        src, dst = [
            (orb_ref.at[:, pl.ds(rows - HALO, HALO)], orb_out.at[0, :, pl.ds(0, HALO)]),
            (local_ref.at[pl.ds(rows - HALO, HALO)], local_out.at[pl.ds(0, HALO)]),
            (orb_out.at[1, :, pl.ds(rows, HALO)], orb_out.at[1, :, pl.ds(0, HALO)]),
        ][k]
        return send(src, dst, edge_sems.at[0, 3 + k], edge_sems.at[1, 3 + k], target)

    @pl.when(has_up)
    def _():
        for k in range(2):
            edge_up(k, ring.up()).start()

    @pl.when(has_down)
    def _():
        for k in range(2):
            edge_down(k, ring.down()).start()

    waves.clear()
    orb_out[0, :, HALO:last] = orb_ref[...]
    local_out[HALO:last] = local_ref[...]

    def clear(start):
        orb_out[:, :, start : start + HALO] = jnp.zeros((2, orbitals, HALO, cells), jnp.float32)
        local_out[start : start + HALO] = jnp.zeros((HALO, cells), jnp.float32)
        trial_out[:, start : start + HALO] = jnp.zeros((half, HALO, cells), jnp.float32)

    @pl.when(jnp.logical_not(has_up))
    def _():
        clear(0)

    @pl.when(jnp.logical_not(has_down))
    def _():
        clear(last)

    def owner_of(q):
        return owner_ref[(ring.side * half + q // per) // kinds]

    def prepare(q):
        cross(q).wait_recv()
        mine = chunk_of(pot_ref.at[ring.side], q, per)[...]
        merged[q] = jnp.where(owner_of(q) == ring.partner, crossed[q], mine)

    def onward(q, came):
        return jnp.where(owner_of(q) // PAIR == ring.line, merged[q], came)

    def halo_up(t, target):
        return send(
            trial_out.at[t, pl.ds(HALO, HALO)], trial_out.at[t, pl.ds(last, HALO)],
            halo_sems.at[0, 0, t], halo_sems.at[1, 0, t], target,
        )

    def halo_down(t, target):
        return send(
            trial_out.at[t, pl.ds(rows, HALO)], trial_out.at[t, pl.ds(0, HALO)],
            halo_sems.at[0, 1, t], halo_sems.at[1, 1, t], target,
        )

    def finish(q):
        place = owner_of(q) // PAIR
        other = jnp.where(place < ring.line, waves.from_left[q], waves.from_right[q])
        value = jnp.where(place == ring.line, merged[q], other)
        chunk_of(trial_out, q, per, HALO)[...] = value

        @pl.when(has_up & (q % per == 0))
        def _():
            halo_up(q // per, ring.up()).start()

        @pl.when(has_down & (q % per == per - 1))
        def _():
            halo_down(q // per, ring.down()).start()

    waves.run(prepare, onward, finish)
    center.wait_recv()

    @pl.when(has_up)
    def _():
        edge_up(2, ring.up()).start()

    @pl.when(has_down)
    def _():
        edge_down(2, ring.down()).start()

    @pl.when(has_up)
    def _():
        for k in range(3):
            edge_up(k, ring.across()).wait_send()
            edge_down(k, ring.across()).wait_recv()
        for t in range(half):
            halo_up(t, ring.across()).wait_send()
            halo_down(t, ring.across()).wait_recv()

    @pl.when(has_down)
    def _():
        for k in range(3):
            edge_down(k, ring.across()).wait_send()
            edge_up(k, ring.across()).wait_recv()
        for t in range(half):
            halo_down(t, ring.across()).wait_send()
            halo_up(t, ring.across()).wait_recv()

    pack.wait()
    center.wait_send()
    for q in range(chunks):
        cross(q).wait_send()
    waves.drain()


def total_kernel(
    count, grids, part_ref, out_ref, from_left, from_right, to_right, to_left, wave_sems, side_sems
):
    ring = Ring(count, grids)
    half, rows, _ = part_ref.shape
    per = rows // HALO
    chunks = half * per
    waves = Waves(ring, chunks, (from_left, from_right, to_right, to_left), wave_sems)
    waves.clear()
    enter(ring, False)
    mine, other = out_ref.at[ring.side], out_ref.at[1 - ring.side]

    def across(view, q):
        part = chunk_of(view, q, per)
        return send(part, part, side_sems.at[0, q], side_sems.at[1, q], ring.across())

    def onward(q, came):
        return came + chunk_of(part_ref, q, per)[...]

    def finish(q):
        total = waves.from_left[q] + chunk_of(part_ref, q, per)[...] + waves.from_right[q]
        chunk_of(mine, q, per)[...] = total
        across(mine, q).start()

    waves.run(lambda q: None, onward, finish)
    for q in range(chunks):
        across(other, q).wait_recv()
        across(mine, q).wait_send()
    waves.drain()


def band_matrix(depth, width):
    k = lax.broadcasted_iota(jnp.int32, (depth, width), 0)
    n = lax.broadcasted_iota(jnp.int32, (depth, width), 1) + width // 2
    far_y, far_z = jnp.abs(k // NZ - n // NZ), jnp.abs(k % NZ - n % NZ)
    near = ((far_y == 1) & (far_z == 0)) | ((far_y == 0) & (far_z == 1))
    far = ((far_y == 2) & (far_z == 0)) | ((far_y == 0) & (far_z == 2))
    return jnp.where(near, 16.0, jnp.where(far, -1.0, 0.0)).astype(jnp.bfloat16)


WIDTH = 256


def sweep_kernel(
    grids, pack_ref, trial_ref, orb_ref, local_ref, out_ref,
    trials, first, scale, now_a, now_b, hi_a, hi_b, lo_a, lo_b, product, density, band, inverse,
    weighted,
):
    n = pl.program_id(0)
    half, planes, cells = trial_ref.shape
    orbitals = orb_ref.shape[1]
    batch = PAIR * half
    rows = planes - 2 * HALO

    @pl.when(n == 0)
    def _():
        band[...] = band_matrix(2 * WIDTH, WIDTH)
        density[...] = jnp.zeros_like(density)
        for x in range(planes):
            trials[x] = jnp.concatenate([trial_ref[:, x, :]] * PAIR, axis=0)

    place = lax.axis_index("grid") * rows - HALO
    where = lax.broadcasted_iota(jnp.int32, (planes, cells), 0) + place
    inside = (where >= 0) & (where < rows * grids)
    for k in range(PAIR):
        diagonal = KINETIC_DIAG + (local_ref[...] + pack_ref[k, pl.ds(n, 1), :])
        inverse[k] = jnp.where(inside, 1.0 / diagonal, 0.0)

    lower = lax.broadcasted_iota(jnp.int32, (batch, cells), 0) < half

    def both(a, b):
        return jnp.where(
            lower, jnp.broadcast_to(a, (batch, cells)), jnp.broadcast_to(b, (batch, cells))
        )

    def split(value):
        high = value.astype(jnp.bfloat16)
        return high, (value - high.astype(jnp.float32)).astype(jnp.bfloat16)

    weight = both(pack_ref[0, pl.ds(orbitals + n, 1), :], pack_ref[1, pl.ds(orbitals + n, 1), :])
    for x in range(0, planes, 2):
        values = []
        for p in (x, x + 1):
            inv = both(inverse[0, pl.ds(p, 1), :], inverse[1, pl.ds(p, 1), :])
            orb = both(orb_ref[0, n, pl.ds(p, 1), :], orb_ref[1, n, pl.ds(p, 1), :])
            scale[p] = inv * (1.0 / 24.0)
            value = -(trials[p] * orb) * inv
            first[p] = value
            values.append(value)
            if HALO <= p < HALO + rows:
                weighted[p - HALO] = weight * orb
        high, low = split(jnp.concatenate(values, axis=0))
        hi_a[x * batch : (x + 2) * batch] = high
        lo_a[x * batch : (x + 2) * batch] = low

    current = first
    buffers = ((now_a, hi_a, lo_a), (now_b, hi_b, lo_b))
    for repeat in range(ITERS):
        hi_in, lo_in = buffers[repeat % 2][1:]
        target, hi_out, lo_out = buffers[(repeat + 1) % 2]
        margin = REACH * (repeat + 1)
        extent = planes - 2 * margin
        for left in range(0, cells, WIDTH):
            a = max(0, left - WIDTH // 2)
            b = min(cells, left + WIDTH + WIDTH // 2)
            k = a - (left - WIDTH // 2)
            weights = band[k : k + b - a, :]
            span = slice(margin * batch, (margin + extent) * batch)
            product[0 : extent * batch] = jnp.dot(
                hi_in[span, a:b], weights, preferred_element_type=jnp.float32
            ) + jnp.dot(lo_in[span, a:b], weights, preferred_element_type=jnp.float32)
            lanes = slice(left, left + WIDTH)
            for x in range(margin, margin + extent, 2):
                values = []
                for p in (x, x + 1):
                    near = current[p - 1, :, lanes] + current[p + 1, :, lanes]
                    far = current[p - 2, :, lanes] + current[p + 2, :, lanes]
                    spot = (p - margin) * batch
                    moved = product[spot : spot + batch] + (16.0 * near - far)
                    value = first[p, :, lanes] + scale[p, :, lanes] * moved
                    if repeat == ITERS - 1:
                        density[p - margin, :, lanes] += weighted[p - margin, :, lanes] * value
                    else:
                        target[p, :, lanes] = value
                        values.append(value)
                if values:
                    high, low = split(jnp.concatenate(values, axis=0))
                    hi_out[x * batch : (x + 2) * batch, lanes] = high
                    lo_out[x * batch : (x + 2) * batch, lanes] = low
        current = target

    @pl.when(n == pl.num_programs(0) - 1)
    def _():
        for x in range(rows):
            out_ref[:, x, :] = density[x, 0:half] + density[x, half:batch]


def shards(count, grids, potentials, orbitals, local_pot, shifts, occupation, owner):
    _, blocks, kinds, rows, cells = potentials.shape
    batch = blocks * kinds
    half = batch // PAIR
    orbital_count = orbitals.shape[0]
    planes = rows + 2 * HALO
    stored = potentials.reshape(PAIR, half, rows, cells)
    vmem = pl.BlockSpec(memory_space=pltpu.VMEM)
    smem = pl.BlockSpec(memory_space=pltpu.SMEM)
    f32 = jnp.float32
    dma = pltpu.SemaphoreType.DMA
    chunks = half * (rows // HALO)
    slots = pltpu.VMEM((chunks, HALO, cells), f32)
    trials, orbs, local, pack = pl.pallas_call(
        functools.partial(spread_kernel, count, grids, kinds),
        out_shape=[
            jax.ShapeDtypeStruct((half, planes, cells), f32),
            jax.ShapeDtypeStruct((PAIR, orbital_count, planes, cells), f32),
            jax.ShapeDtypeStruct((planes, cells), f32),
            jax.ShapeDtypeStruct((PAIR, 2 * orbital_count, cells), f32),
        ],
        in_specs=[smem, smem, smem, vmem, vmem, vmem],
        out_specs=[vmem] * 4,
        scratch_shapes=[
            slots, slots, slots, slots, slots, slots,
            dma((2, chunks)), dma((4, chunks)), dma((2, 2, half)), dma((2, 6)), dma((2, 2)),
        ],
        compiler_params=pltpu.CompilerParams(collective_id=0, has_side_effects=True),
        name="spread",
    )(owner, shifts, occupation, stored, orbitals, local_pot)

    big = pltpu.VMEM((planes, batch, cells), f32)
    packed = pltpu.VMEM((planes * batch, cells), jnp.bfloat16)
    partial = pl.pallas_call(
        functools.partial(sweep_kernel, grids),
        out_shape=jax.ShapeDtypeStruct((half, rows, cells), f32),
        grid=(orbital_count,),
        in_specs=[vmem] * 4,
        out_specs=vmem,
        scratch_shapes=[big, big, big, big, big, packed, packed, packed, packed]
        + [
            pltpu.VMEM((planes * batch, WIDTH), f32),
            pltpu.VMEM((rows, batch, cells), f32),
            pltpu.VMEM((2 * WIDTH, WIDTH), jnp.bfloat16),
            pltpu.VMEM((PAIR, planes, cells), f32),
            pltpu.VMEM((rows, batch, cells), f32),
        ],
        compiler_params=pltpu.CompilerParams(dimension_semantics=("arbitrary",)),
        name="sweeps",
    )(pack, trials, orbs, local)

    totals = pl.pallas_call(
        functools.partial(total_kernel, count, grids),
        out_shape=jax.ShapeDtypeStruct((PAIR, half, rows, cells), f32),
        in_specs=[vmem],
        out_specs=vmem,
        scratch_shapes=[slots, slots, slots, slots, dma((4, chunks)), dma((2, chunks))],
        compiler_params=pltpu.CompilerParams(collective_id=1, has_side_effects=True),
        name="total",
    )(partial)
    owned = (owner == lax.axis_index("orb"))[:, None, None, None]
    return jnp.where(owned, totals.reshape(blocks, kinds, rows, cells), 0.0)[None]


def solution(mesh):
    in_specs = (
        P("orb", None, None, "grid", None),
        P("orb", "grid", None),
        P("grid", None),
        P("orb"),
        P("orb"),
        P(),
    )
    out_specs = P("orb", None, None, "grid", None)
    body = functools.partial(shards, mesh.shape["orb"], mesh.shape["grid"])
    return jax.shard_map(body, mesh=mesh, in_specs=in_specs, out_specs=out_specs, check_vma=False)
```

```python
import functools

import jax
import jax.numpy as jnp
from jax import lax
from jax.experimental import pallas as pl
from jax.experimental.pallas import tpu as pltpu
from jax.sharding import PartitionSpec as P

NZ = 32
ITERS = 4
REACH = 2
HALO = REACH * ITERS
KINETIC_DIAG = 3.75
PAIR = 2
MESH = pl.DeviceIdType.MESH


class Ring:
    def __init__(self, count, grids):
        self.count, self.lines, self.grids = count, count // PAIR, grids
        self.me = lax.axis_index("orb")
        self.row = lax.axis_index("grid")
        self.line, self.side = self.me // PAIR, self.me % PAIR
        self.partner = self.line * PAIR + (1 - self.side)

    def at_line(self, line):
        return {"orb": line * PAIR + self.side, "grid": self.row}

    def across(self):
        return {"orb": self.partner, "grid": self.row}

    def up(self):
        return {"orb": self.me, "grid": self.row - 1}

    def down(self):
        return {"orb": self.me, "grid": self.row + 1}


def enter(ring, with_grid):
    barrier = pltpu.get_barrier_semaphore()
    top = ring.lines - 1

    def greet(target):
        pl.semaphore_signal(barrier, inc=1, device_id=target, device_id_type=MESH)

    greet(ring.across())

    @pl.when(ring.line > 0)
    def _():
        greet(ring.at_line(ring.line - 1))

    @pl.when(ring.line < top)
    def _():
        greet(ring.at_line(ring.line + 1))

    peers = 1 + (ring.line + top) // ring.lines + (2 * top - ring.line) // ring.lines
    if with_grid:

        @pl.when(ring.row > 0)
        def _():
            greet(ring.up())

        @pl.when(ring.row < ring.grids - 1)
        def _():
            greet(ring.down())

        last = ring.grids - 1
        peers = peers + (ring.row + last) // ring.grids + (2 * last - ring.row) // ring.grids
    pl.semaphore_wait(barrier, peers)


def send(src, dst, send_sem, recv_sem, target):
    return pltpu.make_async_remote_copy(
        src_ref=src, dst_ref=dst, send_sem=send_sem, recv_sem=recv_sem,
        device_id=target, device_id_type=MESH,
    )


LAG = 4


class Waves:
    def __init__(self, ring, chunks, buffers, sems):
        self.ring, self.chunks, self.sems = ring, chunks, sems
        self.from_left, self.from_right, self.to_right, self.to_left = buffers
        self.has_left, self.has_right = ring.line > 0, ring.line < ring.lines - 1

    def right(self, q, target):
        sems = self.sems
        return send(self.to_right.at[q], self.from_left.at[q], sems.at[0, q], sems.at[1, q], target)

    def left(self, q, target):
        sems = self.sems
        return send(self.to_left.at[q], self.from_right.at[q], sems.at[2, q], sems.at[3, q], target)

    def clear(self):
        @pl.when(jnp.logical_not(self.has_left))
        def _():
            self.from_left[...] = jnp.zeros_like(self.from_left)

        @pl.when(jnp.logical_not(self.has_right))
        def _():
            self.from_right[...] = jnp.zeros_like(self.from_right)

    def run(self, prepare, onward, finish):
        ring, line, top = self.ring, self.ring.line, self.ring.lines - 1
        beyond = (2 * line) // ring.lines
        late = beyond * line + (1 - beyond) * (top - line)

        def step(s, carry):
            def event(offset, act):
                q = s - offset

                @pl.when((q >= 0) & (q < self.chunks))
                def _():
                    act(q)

            def rightward(q):
                @pl.when(self.has_left)
                def _():
                    self.right(q, ring.across()).wait_recv()

                @pl.when(self.has_right)
                def _():
                    self.to_right[q] = onward(q, self.from_left[q])
                    self.right(q, ring.at_line(line + 1)).start()

            def leftward(q):
                @pl.when(self.has_right)
                def _():
                    self.left(q, ring.across()).wait_recv()

                @pl.when(self.has_left)
                def _():
                    self.to_left[q] = onward(q, self.from_right[q])
                    self.left(q, ring.at_line(line - 1)).start()

            event(0, prepare)
            event(line * LAG, rightward)
            event((top - line) * LAG, leftward)
            event(late * LAG, finish)
            return carry

        lax.fori_loop(0, self.chunks + top * LAG, step, 0)

    def drain(self):
        @pl.when(self.has_right)
        def _():
            for q in range(self.chunks):
                self.right(q, self.ring.across()).wait_send()

        @pl.when(self.has_left)
        def _():
            for q in range(self.chunks):
                self.left(q, self.ring.across()).wait_send()


def chunk_of(ref, q, per, start=0):
    return ref.at[q // per, pl.ds(pl.multiple_of(start + (q % per) * HALO, HALO), HALO)]


def spread_kernel(
    count, grids, kinds, owner_ref, shift_ref, weight_ref, pot_ref, orb_ref, local_ref,
    trial_out, orb_out, local_out, pack_out,
    crossed, merged, from_left, from_right, to_right, to_left,
    cross_sems, wave_sems, halo_sems, edge_sems, pair_sems,
):
    ring = Ring(count, grids)
    orbitals, rows, cells = orb_ref.shape
    half = pot_ref.shape[1]
    per = rows // HALO
    chunks = half * per
    last = HALO + rows
    has_up, has_down = ring.row > 0, ring.row < grids - 1
    waves = Waves(ring, chunks, (from_left, from_right, to_right, to_left), wave_sems)
    for n in range(orbitals):
        pack_out[0, n] = jnp.full((cells,), shift_ref[n], jnp.float32)
        pack_out[0, orbitals + n] = jnp.full((cells,), weight_ref[n].astype(jnp.float32), jnp.float32)
    enter(ring, True)

    def cross(q):
        return send(
            chunk_of(pot_ref.at[1 - ring.side], q, per), crossed.at[q],
            cross_sems.at[0, q], cross_sems.at[1, q], ring.across(),
        )

    for q in range(chunks):
        cross(q).start()
    center = send(
        orb_ref, orb_out.at[1, :, pl.ds(HALO, rows)],
        pair_sems.at[0, 0], pair_sems.at[1, 0], ring.across(),
    )
    center.start()
    pack = send(
        pack_out.at[0], pack_out.at[1], pair_sems.at[0, 1], pair_sems.at[1, 1], ring.across()
    )
    pack.start()

    def edge_up(k, target):
        src, dst = [
            (orb_ref.at[:, pl.ds(0, HALO)], orb_out.at[0, :, pl.ds(last, HALO)]),
            (local_ref.at[pl.ds(0, HALO)], local_out.at[pl.ds(last, HALO)]),
            (orb_out.at[1, :, pl.ds(HALO, HALO)], orb_out.at[1, :, pl.ds(last, HALO)]),
        ][k]
        return send(src, dst, edge_sems.at[0, k], edge_sems.at[1, k], target)

    def edge_down(k, target):
        src, dst = [
            (orb_ref.at[:, pl.ds(rows - HALO, HALO)], orb_out.at[0, :, pl.ds(0, HALO)]),
            (local_ref.at[pl.ds(rows - HALO, HALO)], local_out.at[pl.ds(0, HALO)]),
            (orb_out.at[1, :, pl.ds(rows, HALO)], orb_out.at[1, :, pl.ds(0, HALO)]),
        ][k]
        return send(src, dst, edge_sems.at[0, 3 + k], edge_sems.at[1, 3 + k], target)

    @pl.when(has_up)
    def _():
        for k in range(2):
            edge_up(k, ring.up()).start()

    @pl.when(has_down)
    def _():
        for k in range(2):
            edge_down(k, ring.down()).start()

    waves.clear()
    orb_out[0, :, HALO:last] = orb_ref[...]
    local_out[HALO:last] = local_ref[...]

    def clear(start):
        orb_out[:, :, start : start + HALO] = jnp.zeros((2, orbitals, HALO, cells), jnp.float32)
        local_out[start : start + HALO] = jnp.zeros((HALO, cells), jnp.float32)
        trial_out[:, start : start + HALO] = jnp.zeros((half, HALO, cells), jnp.float32)

    @pl.when(jnp.logical_not(has_up))
    def _():
        clear(0)

    @pl.when(jnp.logical_not(has_down))
    def _():
        clear(last)

    def owner_of(q):
        return owner_ref[(ring.side * half + q // per) // kinds]

    def prepare(q):
        cross(q).wait_recv()
        mine = chunk_of(pot_ref.at[ring.side], q, per)[...]
        merged[q] = jnp.where(owner_of(q) == ring.partner, crossed[q], mine)

    def onward(q, came):
        return jnp.where(owner_of(q) // PAIR == ring.line, merged[q], came)

    def halo_up(t, target):
        return send(
            trial_out.at[t, pl.ds(HALO, HALO)], trial_out.at[t, pl.ds(last, HALO)],
            halo_sems.at[0, 0, t], halo_sems.at[1, 0, t], target,
        )

    def halo_down(t, target):
        return send(
            trial_out.at[t, pl.ds(rows, HALO)], trial_out.at[t, pl.ds(0, HALO)],
            halo_sems.at[0, 1, t], halo_sems.at[1, 1, t], target,
        )

    def finish(q):
        place = owner_of(q) // PAIR
        other = jnp.where(place < ring.line, waves.from_left[q], waves.from_right[q])
        value = jnp.where(place == ring.line, merged[q], other)
        chunk_of(trial_out, q, per, HALO)[...] = value

        @pl.when(has_up & (q % per == 0))
        def _():
            halo_up(q // per, ring.up()).start()

        @pl.when(has_down & (q % per == per - 1))
        def _():
            halo_down(q // per, ring.down()).start()

    waves.run(prepare, onward, finish)
    center.wait_recv()

    @pl.when(has_up)
    def _():
        edge_up(2, ring.up()).start()

    @pl.when(has_down)
    def _():
        edge_down(2, ring.down()).start()

    @pl.when(has_up)
    def _():
        for k in range(3):
            edge_up(k, ring.across()).wait_send()
            edge_down(k, ring.across()).wait_recv()
        for t in range(half):
            halo_up(t, ring.across()).wait_send()
            halo_down(t, ring.across()).wait_recv()

    @pl.when(has_down)
    def _():
        for k in range(3):
            edge_down(k, ring.across()).wait_send()
            edge_up(k, ring.across()).wait_recv()
        for t in range(half):
            halo_down(t, ring.across()).wait_send()
            halo_up(t, ring.across()).wait_recv()

    pack.wait()
    center.wait_send()
    for q in range(chunks):
        cross(q).wait_send()
    waves.drain()


def total_kernel(
    count, grids, part_ref, out_ref, from_left, from_right, to_right, to_left, wave_sems, side_sems
):
    ring = Ring(count, grids)
    half, rows, _ = part_ref.shape
    per = rows // HALO
    chunks = half * per
    waves = Waves(ring, chunks, (from_left, from_right, to_right, to_left), wave_sems)
    waves.clear()
    enter(ring, False)
    mine, other = out_ref.at[ring.side], out_ref.at[1 - ring.side]

    def across(view, q):
        part = chunk_of(view, q, per)
        return send(part, part, side_sems.at[0, q], side_sems.at[1, q], ring.across())

    def onward(q, came):
        return came + chunk_of(part_ref, q, per)[...]

    def finish(q):
        total = waves.from_left[q] + chunk_of(part_ref, q, per)[...] + waves.from_right[q]
        chunk_of(mine, q, per)[...] = total
        across(mine, q).start()

    waves.run(lambda q: None, onward, finish)
    for q in range(chunks):
        across(other, q).wait_recv()
        across(mine, q).wait_send()
    waves.drain()


def band_matrix(depth, width):
    k = lax.broadcasted_iota(jnp.int32, (depth, width), 0)
    n = lax.broadcasted_iota(jnp.int32, (depth, width), 1) + width // 2
    far_y, far_z = jnp.abs(k // NZ - n // NZ), jnp.abs(k % NZ - n % NZ)
    near = ((far_y == 1) & (far_z == 0)) | ((far_y == 0) & (far_z == 1))
    far = ((far_y == 2) & (far_z == 0)) | ((far_y == 0) & (far_z == 2))
    return jnp.where(near, 16.0, jnp.where(far, -1.0, 0.0)).astype(jnp.bfloat16)


WIDTH = 256


def sweep_kernel(
    grids, pack_ref, trial_ref, orb_ref, local_ref, out_ref,
    trials, first, scale, now_a, now_b, hi_a, hi_b, lo_a, lo_b, product, density, band, inverse,
    weighted,
):
    n = pl.program_id(0)
    half, planes, cells = trial_ref.shape
    orbitals = orb_ref.shape[1]
    batch = PAIR * half
    rows = planes - 2 * HALO

    @pl.when(n == 0)
    def _():
        band[...] = band_matrix(2 * WIDTH, WIDTH)
        density[...] = jnp.zeros_like(density)
        for x in range(planes):
            trials[x] = jnp.concatenate([trial_ref[:, x, :]] * PAIR, axis=0)

    place = lax.axis_index("grid") * rows - HALO
    where = lax.broadcasted_iota(jnp.int32, (planes, cells), 0) + place
    inside = (where >= 0) & (where < rows * grids)
    for k in range(PAIR):
        diagonal = KINETIC_DIAG + (local_ref[...] + pack_ref[k, pl.ds(n, 1), :])
        inverse[k] = jnp.where(inside, 1.0 / diagonal, 0.0)

    lower = lax.broadcasted_iota(jnp.int32, (batch, cells), 0) < half

    def both(a, b):
        return jnp.where(
            lower, jnp.broadcast_to(a, (batch, cells)), jnp.broadcast_to(b, (batch, cells))
        )

    def split(value):
        high = value.astype(jnp.bfloat16)
        return high, (value - high.astype(jnp.float32)).astype(jnp.bfloat16)

    weight = both(pack_ref[0, pl.ds(orbitals + n, 1), :], pack_ref[1, pl.ds(orbitals + n, 1), :])
    for x in range(0, planes, 2):
        values = []
        for p in (x, x + 1):
            inv = both(inverse[0, pl.ds(p, 1), :], inverse[1, pl.ds(p, 1), :])
            orb = both(orb_ref[0, n, pl.ds(p, 1), :], orb_ref[1, n, pl.ds(p, 1), :])
            scale[p] = inv * (1.0 / 24.0)
            value = -(trials[p] * orb) * inv
            first[p] = value
            values.append(value)
            if HALO <= p < HALO + rows:
                weighted[p - HALO] = weight * orb
        high, low = split(jnp.concatenate(values, axis=0))
        hi_a[x * batch : (x + 2) * batch] = high
        lo_a[x * batch : (x + 2) * batch] = low

    current = first
    buffers = ((now_a, hi_a, lo_a), (now_b, hi_b, lo_b))
    for repeat in range(ITERS):
        hi_in, lo_in = buffers[repeat % 2][1:]
        target, hi_out, lo_out = buffers[(repeat + 1) % 2]
        margin = REACH * (repeat + 1)
        extent = planes - 2 * margin
        for left in range(0, cells, WIDTH):
            a = max(0, left - WIDTH // 2)
            b = min(cells, left + WIDTH + WIDTH // 2)
            k = a - (left - WIDTH // 2)
            weights = band[k : k + b - a, :]
            span = slice(margin * batch, (margin + extent) * batch)
            product[0 : extent * batch] = jnp.dot(
                hi_in[span, a:b], weights, preferred_element_type=jnp.float32
            ) + jnp.dot(lo_in[span, a:b], weights, preferred_element_type=jnp.float32)
            lanes = slice(left, left + WIDTH)
            for x in range(margin, margin + extent, 2):
                values = []
                for p in (x, x + 1):
                    near = current[p - 1, :, lanes] + current[p + 1, :, lanes]
                    far = current[p - 2, :, lanes] + current[p + 2, :, lanes]
                    spot = (p - margin) * batch
                    moved = product[spot : spot + batch] + (16.0 * near - far)
                    value = first[p, :, lanes] + scale[p, :, lanes] * moved
                    if repeat == ITERS - 1:
                        density[p - margin, :, lanes] += weighted[p - margin, :, lanes] * value
                    else:
                        target[p, :, lanes] = value
                        values.append(value)
                if values:
                    high, low = split(jnp.concatenate(values, axis=0))
                    hi_out[x * batch : (x + 2) * batch, lanes] = high
                    lo_out[x * batch : (x + 2) * batch, lanes] = low
        current = target

    @pl.when(n == pl.num_programs(0) - 1)
    def _():
        for x in range(rows):
            out_ref[:, x, :] = density[x, 0:half] + density[x, half:batch]


def own_kernel(owner_ref, total_ref, out_ref):
    for b in range(total_ref.shape[0]):
        out_ref[b] = jnp.where(owner_ref[b] == lax.axis_index("orb"), total_ref[b], 0.0)


def shards(count, grids, potentials, orbitals, local_pot, shifts, occupation, owner):
    _, blocks, kinds, rows, cells = potentials.shape
    batch = blocks * kinds
    half = batch // PAIR
    orbital_count = orbitals.shape[0]
    planes = rows + 2 * HALO
    stored = potentials.reshape(PAIR, half, rows, cells)
    vmem = pl.BlockSpec(memory_space=pltpu.VMEM)
    smem = pl.BlockSpec(memory_space=pltpu.SMEM)
    f32 = jnp.float32
    dma = pltpu.SemaphoreType.DMA
    chunks = half * (rows // HALO)
    slots = pltpu.VMEM((chunks, HALO, cells), f32)
    trials, orbs, local, pack = pl.pallas_call(
        functools.partial(spread_kernel, count, grids, kinds),
        out_shape=[
            jax.ShapeDtypeStruct((half, planes, cells), f32),
            jax.ShapeDtypeStruct((PAIR, orbital_count, planes, cells), f32),
            jax.ShapeDtypeStruct((planes, cells), f32),
            jax.ShapeDtypeStruct((PAIR, 2 * orbital_count, cells), f32),
        ],
        in_specs=[smem, smem, smem, vmem, vmem, vmem],
        out_specs=[vmem] * 4,
        scratch_shapes=[
            slots, slots, slots, slots, slots, slots,
            dma((2, chunks)), dma((4, chunks)), dma((2, 2, half)), dma((2, 6)), dma((2, 2)),
        ],
        compiler_params=pltpu.CompilerParams(collective_id=0, has_side_effects=True),
        name="spread",
    )(owner, shifts, occupation, stored, orbitals, local_pot)

    big = pltpu.VMEM((planes, batch, cells), f32)
    packed = pltpu.VMEM((planes * batch, cells), jnp.bfloat16)
    partial = pl.pallas_call(
        functools.partial(sweep_kernel, grids),
        out_shape=jax.ShapeDtypeStruct((half, rows, cells), f32),
        grid=(orbital_count,),
        in_specs=[vmem] * 4,
        out_specs=vmem,
        scratch_shapes=[big, big, big, big, big, packed, packed, packed, packed]
        + [
            pltpu.VMEM((planes * batch, WIDTH), f32),
            pltpu.VMEM((rows, batch, cells), f32),
            pltpu.VMEM((2 * WIDTH, WIDTH), jnp.bfloat16),
            pltpu.VMEM((PAIR, planes, cells), f32),
            pltpu.VMEM((rows, batch, cells), f32),
        ],
        compiler_params=pltpu.CompilerParams(dimension_semantics=("arbitrary",)),
        name="sweeps",
    )(pack, trials, orbs, local)

    totals = pl.pallas_call(
        functools.partial(total_kernel, count, grids),
        out_shape=jax.ShapeDtypeStruct((PAIR, half, rows, cells), f32),
        in_specs=[vmem],
        out_specs=vmem,
        scratch_shapes=[slots, slots, slots, slots, dma((4, chunks)), dma((2, chunks))],
        compiler_params=pltpu.CompilerParams(collective_id=1, has_side_effects=True),
        name="total",
    )(partial)
    response = pl.pallas_call(
        own_kernel,
        out_shape=jax.ShapeDtypeStruct((blocks, kinds, rows, cells), f32),
        in_specs=[smem, vmem],
        out_specs=vmem,
        name="own",
    )(owner, totals.reshape(blocks, kinds, rows, cells))
    return response[None]


def solution(mesh):
    in_specs = (
        P("orb", None, None, "grid", None),
        P("orb", "grid", None),
        P("grid", None),
        P("orb"),
        P("orb"),
        P(),
    )
    out_specs = P("orb", None, None, "grid", None)
    body = functools.partial(shards, mesh.shape["orb"], mesh.shape["grid"])
    return jax.shard_map(body, mesh=mesh, in_specs=in_specs, out_specs=out_specs, check_vma=False)
```
